512 devices in a mesh: res: 32 (over x, y_hi, core), prog: 16 (over y_lo, z).
Axes of the slice: x: 4, y: 8 (y_hi: 4, y_lo: 2; y = y_hi * 2 + y_lo), z: 8, core: 2. Of those that a mesh axis runs over, the one named last changes fastest.
Arguments:
- queries: bfloat16 [1024, 32768], P('res', 'prog'), may hold values from -14 to 14
- key_vectors: bfloat16 [1024, 32768], P('res', 'prog'), may hold values from -14 to 14
- values: bfloat16 [1024, 32768], P('res', 'prog'), may hold values from -6 to 6
- cotangent: bfloat16 [1024, 32768], P('res', 'prog'), may hold values from -6 to 6
- eligible: int32 [1024, 1024], P('res', 'prog'), may hold values from 0 to 1, as said below
Outputs:
- grad_queries: float32 [1024, 32768], P('res', 'prog')
- grad_keys: float32 [1024, 32768], P('res', 'prog')
- grad_values: float32 [1024, 32768], P('res', 'prog')
The draws below stay inside these ranges and needn't reach their ends.
Inputs may be any that keep to these rules, and one draw needn't show every extreme that they name: Every resident has at least one eligible program and every program at least one eligible resident.
All inputs are finite; a program needn't handle non-finite values.
Results may differ from the reference program's by a relative error of at most 0.0075.
Values may be sent and summed in bfloat16 or wider, within the bound.
No kernel may reach another device: no remote copies, remote signals or barrier semaphores. Data moves between devices by JAX's collectives and lax.ppermute only.
A program may use at most 64 MiB of HBM per device.

```python
import math
import jax
import jax.numpy as jnp
from jax import lax

CH = 32
RES = 1024
PROG = 1024


plant_count = 8


def plant_sites(key):
    site_key = jax.random.fold_in(key, 101)
    first_key, second_key = jax.random.split(site_key)
    plant_rows = 4 * jax.random.permutation(first_key, RES // 4)[:plant_count]
    plant_cols = jax.random.randint(second_key, (plant_count,), 0, PROG)
    return (plant_rows.astype(jnp.int32), plant_cols.astype(jnp.int32))


def draw_eligible(key, part):
    density = jax.random.randint(jax.random.fold_in(key, 1), (RES // 32, PROG // 32), 0, 17)
    rolls = jax.random.randint(jax.random.fold_in(key, 2), (RES, PROG), 0, 16)
    row_iota = jnp.arange(RES, dtype=jnp.int32)
    col_iota = jnp.arange(PROG, dtype=jnp.int32)
    level = density[(row_iota // 32)[:, None], (col_iota // 32)[None, :]]
    chosen = rolls < level
    sigma = jax.random.permutation(jax.random.fold_in(key, 3), PROG).astype(jnp.int32)
    tau = jax.random.permutation(jax.random.fold_in(key, 4), RES).astype(jnp.int32)
    chosen = chosen | (col_iota[None, :] == sigma[row_iota % PROG][:, None])
    chosen = chosen | (row_iota[:, None] == tau[col_iota % RES][None, :])
    plant_rows, plant_cols = plant_sites(key)
    chosen = chosen.at[plant_rows, (plant_cols + 1) % PROG].set(True)
    chosen = chosen.at[plant_rows, (plant_cols + 2) % PROG].set(True)
    chosen = chosen.at[plant_rows + 1, plant_cols].set(True)
    chosen = chosen.at[plant_rows + 2, plant_cols].set(True)
    return chosen.astype(jnp.int32)


def queries_and_keys(key):
    shape_cube = (RES, PROG, CH)
    query_cube = jax.random.truncated_normal(jax.random.fold_in(key, 7), -4.0, 4.0, shape_cube, jnp.float32)
    key_cube = jax.random.truncated_normal(jax.random.fold_in(key, 8), -4.0, 4.0, shape_cube, jnp.float32)
    return (query_cube.reshape(RES, PROG * CH), key_cube.reshape(RES, PROG * CH))


def draw_queries(key, part):
    return queries_and_keys(key)[0].astype(jnp.bfloat16)


def draw_key_vectors(key, part):
    return queries_and_keys(key)[1].astype(jnp.bfloat16)


def levels(own_key, extent, pieces, smallest, largest):
    loudness = 1.0
    for position, parts in pieces:
        heights = jax.random.uniform(jax.random.fold_in(jax.random.fold_in(own_key, 6), position), (parts,), jnp.float32, smallest / len(pieces), largest / len(pieces))
        loudness = loudness * jnp.repeat(jnp.exp(heights), extent[position] // parts).reshape((-1,) + (1,) * (len(extent) - 1 - position))
    return loudness


def normal_values(own_key, shape, deviation, bound, pieces=(), kind=jnp.bfloat16):
    array = jax.random.normal(own_key, shape, jnp.float32) * deviation
    if len(pieces) > 0:
        array = levels(own_key, shape, pieces, -0.22, 0.18) * array
    return jnp.clip(array, min=-bound, max=bound).astype(kind)


def setup_inputs(seed: int = 0) -> dict:
    key_list = jax.random.split(jax.random.key(seed), 6)
    return {
        "queries": draw_queries(jax.random.fold_in(key_list[5], 71), 0),
        "key_vectors": draw_key_vectors(jax.random.fold_in(key_list[5], 71), 0),
        "values": normal_values(key_list[2], (RES, PROG * CH), 1.0, 6.0, ((0, 32), (1, 16))),
        "cotangent": normal_values(key_list[3], (RES, PROG * CH), 1.0, 6.0, ((0, 32), (1, 16))),
        "eligible": draw_eligible(jax.random.fold_in(key_list[5], 71), 0),
    }


masked_score = -1e+30

def block_grads(query_block, cot_block, key_rows, value_rows, eligible_keys, score_scale):
    scores = jnp.dot(query_block, key_rows.T, preferred_element_type=jnp.float32) * score_scale
    scores = jnp.where(eligible_keys[None, :], scores, masked_score)
    row_max = lax.optimization_barrier(jnp.max(scores, axis=1, keepdims=True))
    expo = jnp.exp(scores - row_max)
    weights = expo / lax.optimization_barrier(jnp.sum(expo, axis=1, keepdims=True))
    weights_low = weights.astype(jnp.bfloat16)
    outputs = jnp.dot(weights_low, value_rows, preferred_element_type=jnp.float32)
    weight_grad = jnp.dot(cot_block, value_rows.T, preferred_element_type=jnp.float32)
    delta = lax.optimization_barrier(jnp.sum(cot_block.astype(jnp.float32) * outputs, axis=1, keepdims=True))
    score_grad = (weights * (weight_grad - delta) * score_scale).astype(jnp.bfloat16)
    query_grad = jnp.dot(score_grad, key_rows, preferred_element_type=jnp.float32)
    dims = (((0,), (0,)), ((), ()))
    key_grad = lax.dot_general(score_grad, query_block, dims, preferred_element_type=jnp.float32)
    value_grad = lax.dot_general(weights_low, cot_block, dims, preferred_element_type=jnp.float32)
    return (query_grad, key_grad, value_grad)

def pass_grads(queries, key_cube, value_cube, cot_cube, eligible_keys, item_axis):
    item_count = queries.shape[item_axis]
    length = queries.shape[1 - item_axis]
    channels = queries.shape[2]
    block_rows = min(512, length)
    block_count = length // block_rows
    score_scale = 1.0 / math.sqrt(channels)
    offsets = jnp.arange(block_count, dtype=jnp.int32) * block_rows

    def item_body(item_index, running):
        out_queries, out_keys, out_values = running
        query_item = lax.dynamic_index_in_dim(queries, item_index, item_axis, keepdims=False)
        key_item = lax.dynamic_index_in_dim(key_cube, item_index, item_axis, keepdims=False)
        value_item = lax.dynamic_index_in_dim(value_cube, item_index, item_axis, keepdims=False)
        cot_item = lax.dynamic_index_in_dim(cot_cube, item_index, item_axis, keepdims=False)
        keep_item = lax.dynamic_index_in_dim(eligible_keys, item_index, item_axis, keepdims=False)

        def block_step(partial_value, offset):
            key_sum, value_sum = partial_value
            query_block = lax.dynamic_slice_in_dim(query_item, offset, block_rows, 0)
            cot_block = lax.dynamic_slice_in_dim(cot_item, offset, block_rows, 0)
            query_grad, key_grad, value_grad = block_grads(query_block, cot_block, key_item, value_item, keep_item, score_scale)
            return ((key_sum + key_grad, value_sum + value_grad), query_grad.astype(jnp.bfloat16))
        zero_sums = (jnp.zeros((length, channels), jnp.float32), jnp.zeros((length, channels), jnp.float32))
        (key_sum, value_sum), query_blocks = lax.scan(block_step, zero_sums, offsets)
        query_total = query_blocks.reshape(length, channels)
        out_queries = lax.dynamic_update_index_in_dim(out_queries, query_total, item_index, item_axis)
        out_keys = lax.dynamic_update_index_in_dim(out_keys, key_sum.astype(jnp.bfloat16), item_index, item_axis)
        out_values = lax.dynamic_update_index_in_dim(out_values, value_sum.astype(jnp.bfloat16), item_index, item_axis)
        return (out_queries, out_keys, out_values)
    empty = jnp.zeros(queries.shape, jnp.bfloat16)
    return lax.fori_loop(0, item_count, item_body, (empty, empty, empty))

def reference(queries, key_vectors, values, cotangent, eligible):
    shape_cube = (RES, PROG, CH)
    query_cube = queries.reshape(shape_cube)
    key_cube = key_vectors.reshape(shape_cube)
    value_cube = values.reshape(shape_cube)
    cot_cube = cotangent.reshape(shape_cube)
    eligible_keys = eligible > 0
    row_grads = pass_grads(query_cube, key_cube, value_cube, cot_cube, eligible_keys, 0)
    col_grads = pass_grads(query_cube, key_cube, value_cube, cot_cube, eligible_keys, 1)
    totals = [(row_grads[slot].astype(jnp.float32) + col_grads[slot].astype(jnp.float32)).reshape(RES, PROG * CH) for slot in range(3)]
    return (totals[0], totals[1], totals[2])
```

```python
import functools
import math

import jax
import jax.numpy as jnp
from jax import lax
from jax.experimental import pallas as pl
from jax.experimental.pallas import tpu as pltpu
from jax.sharding import PartitionSpec as P

CH = 32
LANES = 128
BLOCKS = LANES // CH
SCALE = 1.0 / math.sqrt(CH)
EXP2_SCALE = SCALE * math.log2(math.e)
masked_score = -1e30
INTERPRET = False
QB = 256
KEYS = 1024
KC = 256

f32 = jnp.float32
bf16 = jnp.bfloat16


def iota(shape, dim):
    return lax.broadcasted_iota(jnp.int32, shape, dim)


def dot(x, y, cx=1, cy=0):
    return lax.dot_general(x, y, (((cx,), (cy,)), ((), ())), preferred_element_type=f32)


def call(body, outs, scratch, *args):
    return pl.pallas_call(
        body,
        out_shape=outs,
        in_specs=[pl.BlockSpec(memory_space=pltpu.VMEM)] * len(args),
        out_specs=jax.tree.map(lambda _: pl.BlockSpec(memory_space=pltpu.VMEM), outs),
        scratch_shapes=scratch,
        interpret=INTERPRET,
        compiler_params=pltpu.CompilerParams(vmem_limit_bytes=48 * 2**20),
    )(*args)


def pack_rows_body(q_ref, k_ref, v_ref, g_ref, e_ref, out_ref, scr_ref):
    for t, ref in enumerate((q_ref, k_ref, v_ref, g_ref)):
        for l in range(16):
            scr_ref[t, pl.ds(l, 32, stride=16), :] = ref[:, l * LANES : (l + 1) * LANES].astype(f32)
    for t in range(4):
        out_ref[:, t * 32 : (t + 1) * 32, :] = scr_ref[t].reshape(16, 32, LANES).astype(bf16)
    keep = e_ref[...].astype(f32).astype(bf16)
    halves = [
        dot((iota((16, 32), 1) == 2 * iota((16, 32), 0) + s).astype(f32).astype(bf16), keep)
        for s in range(2)
    ]
    plane = jnp.concatenate(halves, axis=1)
    for j in range(16):
        out_ref[j, 128:136, :] = jnp.broadcast_to(plane[j : j + 1, :], (8, LANES)).astype(bf16)


def pack_cols_body(q_ref, k_ref, v_ref, g_ref, e_ref, out_ref):
    low = iota((16, LANES), 1) < 64
    for t, ref in enumerate((q_ref, k_ref, v_ref, g_ref)):
        for l in range(16):
            a = ref[0:16, l * LANES : (l + 1) * LANES].astype(f32)
            b = ref[16:32, l * LANES : (l + 1) * LANES].astype(f32)
            first = jnp.where(low, a, pltpu.roll(b, 64, 1))
            second = jnp.where(low, pltpu.roll(a, 64, 1), b)
            out_ref[2 * l, t * 16 : (t + 1) * 16, :] = first.astype(bf16)
            out_ref[2 * l + 1, t * 16 : (t + 1) * 16, :] = second.astype(bf16)
    keep = e_ref[...].astype(f32).astype(bf16)
    parts = [
        dot((iota((32, 64), 1) == 2 * iota((32, 64), 0) + pp).astype(f32).astype(bf16), keep, 1, 1)
        for pp in range(2)
    ]
    plane = jnp.concatenate(parts + [jnp.zeros((32, 64), f32)], axis=1)
    for i in range(32):
        out_ref[i, 64:72, :] = jnp.broadcast_to(plane[i : i + 1, :], (8, LANES)).astype(bf16)


def attend_body(rows, in_ref, out_ref, qx, gx, kx, kt, vx, dqt, dk, dv, st, da):
    peers = 16 if rows else 32
    items = 2 if rows else 1
    group = 256 if rows else 512
    turns = 4 if rows else 2
    turn = LANES // turns
    tensor_rows = 32 if rows else 16
    plane = in_ref[:, 4 * tensor_rows, :]
    lane = iota((group, LANES), 1)
    sub = iota((group, LANES), 0) % 16
    for item in range(items):
        parts = []
        for t in range(4):
            first = t * tensor_rows + item * 16
            parts.append(in_ref[:, first : first + 16, :].reshape(group, LANES).astype(f32))
        q4, k4, v4, g4 = parts
        spread = (iota((group, peers), 0) // 16 == iota((group, peers), 1)).astype(f32).astype(bf16)
        barred = 1.0 - dot(spread, plane)
        src, dst = iota((LANES, LANES), 0), iota((LANES, LANES), 1)
        if rows:
            here = lane // 4 == item * 16 + sub
            place = dst == CH * (src % 4)
        else:
            here = (lane % 16 == sub) & (lane < 64)
            place = dst == 64 * ((src // 16) % 2) + 32 * (src // 32)
        mark = jnp.where(here, barred, 0.0).astype(bf16)
        bias = dot(mark, place.astype(f32).astype(bf16)) * masked_score
        kt4 = k4.T
        for d in range(turns):
            span = slice(d * group, (d + 1) * group)

            def turned(x):
                return pltpu.roll(x, turn * d, 1) if d else x

            kx[item, span, 0:LANES] = turned(k4).astype(bf16)
            kx[item, span, LANES : 2 * LANES] = turned(bias).astype(bf16)
            vx[item, span, :] = turned(v4).astype(bf16)
            for a in range(BLOCKS):
                b = (a - d * turn // CH) % BLOCKS
                kt[item, a, :, span] = kt4[b * CH : (b + 1) * CH, :].astype(bf16)
        for a in range(BLOCKS):
            mine = lane // CH == a
            qa = jnp.where(mine, q4, 0.0).astype(bf16)
            ga = jnp.where(mine, g4, 0.0).astype(bf16)
            pick = (iota((QB, LANES), 1) == a * CH).astype(f32).astype(bf16)
            for part in range(group // QB):
                step = (item + part) * BLOCKS + a
                qx[step, :, 0:LANES] = qa[part * QB : (part + 1) * QB, :]
                qx[step, :, LANES : 2 * LANES] = pick
                gx[step] = ga[part * QB : (part + 1) * QB, :]
    dk[...] = jnp.zeros(dk.shape, f32)
    dv[...] = jnp.zeros(dv.shape, f32)
    chunks = [slice(c * KC, (c + 1) * KC) for c in range(KEYS // KC)]

    def one_step(step, carry):
        item = step // BLOCKS if rows else 0
        block = step % BLOCKS
        q = qx[step]
        g = gx[step]
        top = jnp.full((8, QB), -jnp.inf, f32)
        for c in chunks:
            s = dot(kx[item, c, :], q, 1, 1)
            st[c, :] = s
            top = jnp.maximum(top, jnp.max(s.reshape(KC // 8, 8, QB), axis=0))
            da[c, :] = dot(vx[item, c, :], g, 1, 1)
        top = jnp.max(top, axis=0, keepdims=True)
        total = jnp.zeros((8, QB), f32)
        inner = jnp.zeros((8, QB), f32)
        for c in chunks:
            e = jnp.exp2((st[c, :] - top) * EXP2_SCALE)
            st[c, :] = e
            total += jnp.sum(e.reshape(KC // 8, 8, QB), axis=0)
            inner += jnp.sum((e * da[c, :]).reshape(KC // 8, 8, QB), axis=0)
        inverse = 1.0 / jnp.sum(total, axis=0, keepdims=True)
        delta = jnp.sum(inner, axis=0, keepdims=True) * inverse
        dq = jnp.zeros((CH, QB), f32)
        for c in chunks:
            w = st[c, :] * inverse
            ds = (w * (da[c, :] - delta)).astype(bf16)
            dv[item, c, :] += dot(w.astype(bf16), g)
            dk[item, c, :] += dot(ds, q[:, 0:LANES])
            dq += dot(kt[item, block, :, c], ds)
        dqt[step] = dq
        return carry

    lax.fori_loop(0, 8, one_step, 0)

    for item in range(items):
        dq4 = [
            dqt[(item + part) * BLOCKS : (item + part + 1) * BLOCKS].reshape(LANES, QB).T
            for part in range(group // QB)
        ]
        sums = [jnp.concatenate(dq4, axis=0) * SCALE if len(dq4) > 1 else dq4[0] * SCALE]
        for acc, factor in ((dk, SCALE), (dv, 1.0)):
            total = acc[item, 0:group, :]
            for d in range(1, turns):
                total += pltpu.roll(acc[item, d * group : (d + 1) * group, :], LANES - turn * d, 1)
            sums.append(total * factor)
        for t in range(3):
            first = t * tensor_rows + item * 16
            out_ref[:, first : first + 16, :] = sums[t].reshape(peers, 16, LANES).astype(bf16)


def attend(rows, received):
    items = 2 if rows else 1
    peers = 16 if rows else 32
    scratch = [
        pltpu.VMEM((8, QB, 2 * LANES), bf16),
        pltpu.VMEM((8, QB, LANES), bf16),
        pltpu.VMEM((items, KEYS, 2 * LANES), bf16),
        pltpu.VMEM((items, BLOCKS, CH, KEYS), bf16),
        pltpu.VMEM((items, KEYS, LANES), bf16),
        pltpu.VMEM((8, CH, QB), f32),
        pltpu.VMEM((items, KEYS, LANES), f32),
        pltpu.VMEM((items, KEYS, LANES), f32),
        pltpu.VMEM((KEYS, QB), f32),
        pltpu.VMEM((KEYS, QB), f32),
    ]
    out = jax.ShapeDtypeStruct((peers, 96 if rows else 48, LANES), bf16)
    return call(functools.partial(attend_body, rows), out, scratch, received)


def unpack_rows_body(in_ref, out_ref, scr_ref):
    for t in range(3):
        scr_ref[t] = in_ref[:, t * 32 : (t + 1) * 32, :].reshape(512, LANES).astype(f32)
    for t in range(3):
        for l in range(16):
            out_ref[t, :, l * LANES : (l + 1) * LANES] = scr_ref[t, pl.ds(l, 32, stride=16), :]


def finish_body(rows_ref, in_ref, q_ref, k_ref, v_ref):
    low = iota((16, LANES), 1) < 64
    for t, ref in enumerate((q_ref, k_ref, v_ref)):
        for l in range(16):
            cols = slice(l * LANES, (l + 1) * LANES)
            a = in_ref[2 * l, t * 16 : (t + 1) * 16, :].astype(f32)
            b = in_ref[2 * l + 1, t * 16 : (t + 1) * 16, :].astype(f32)
            ref[0:16, cols] = rows_ref[t, 0:16, cols] + jnp.where(low, a, pltpu.roll(b, 64, 1))
            ref[16:32, cols] = rows_ref[t, 16:32, cols] + jnp.where(low, pltpu.roll(a, 64, 1), b)


def exchange(array, axis):
    return lax.all_to_all(array, axis, split_axis=0, concat_axis=0, tiled=True)


def pack_rows(*args):
    out = jax.ShapeDtypeStruct((16, 136, LANES), bf16)
    return call(pack_rows_body, out, [pltpu.VMEM((4, 512, LANES), f32)], *args)


def pack_cols(*args):
    return call(pack_cols_body, jax.ShapeDtypeStruct((32, 72, LANES), bf16), [], *args)


def unpack_rows(array):
    out = jax.ShapeDtypeStruct((3, 32, 2048), f32)
    return call(unpack_rows_body, out, [pltpu.VMEM((3, 512, LANES), f32)], array)


def finish(row_part, array):
    return call(finish_body, [jax.ShapeDtypeStruct((32, 2048), f32)] * 3, [], row_part, array)


def per_device(*args):
    row_in = exchange(pack_rows(*args), "prog")
    col_in = exchange(pack_cols(*args), "res")
    row_out = exchange(attend(True, row_in), "prog")
    col_out = exchange(attend(False, col_in), "res")
    return tuple(finish(unpack_rows(row_out), col_out))


def solution(mesh):
    return jax.shard_map(
        per_device,
        mesh=mesh,
        in_specs=(P("res", "prog"),) * 5,
        out_specs=(P("res", "prog"),) * 3,
        check_vma=False,
    )
```

```python
import functools
import math

import jax
import jax.numpy as jnp
from jax import lax
from jax.experimental import pallas as pl
from jax.experimental.pallas import tpu as pltpu
from jax.sharding import PartitionSpec as P

CH = 32
LANES = 128
BLOCKS = LANES // CH
SCALE = 1.0 / math.sqrt(CH)
EXP2_SCALE = SCALE * math.log2(math.e)
masked_score = -1e30
INTERPRET = False
QB = 256
KEYS = 1024
KC = 256
TURNS = 4

f32 = jnp.float32
bf16 = jnp.bfloat16


def iota(shape, dim):
    return lax.broadcasted_iota(jnp.int32, shape, dim)


def dot(x, y, cx=1, cy=0):
    return lax.dot_general(x, y, (((cx,), (cy,)), ((), ())), preferred_element_type=f32)


def call(body, outs, scratch, *args, spaces=None):
    return pl.pallas_call(
        body,
        out_shape=outs,
        in_specs=[pl.BlockSpec(memory_space=m) for m in spaces or [pltpu.VMEM] * len(args)],
        out_specs=jax.tree.map(lambda _: pl.BlockSpec(memory_space=pltpu.VMEM), outs),
        scratch_shapes=scratch,
        interpret=INTERPRET,
        compiler_params=pltpu.CompilerParams(vmem_limit_bytes=48 * 2**20),
    )(*args)


def pack_body(x_ref, *refs):
    hbm, e_hbm, rows_ref, cols_refs = refs[:4], refs[4], refs[5], refs[6:10]
    bufs, e_ref, scr_ref, sems = refs[10:]
    copies = [pltpu.make_async_copy(hbm[t], bufs.at[t], sems.at[t]) for t in range(4)]
    copies.append(pltpu.make_async_copy(e_hbm, e_ref, sems.at[4]))
    for copy in copies:
        copy.start()
    x = x_ref[0]
    low = iota((16, LANES), 1) < 64
    for t in range(4):
        copies[t].wait()
        for l in range(16):
            scr_ref[t, pl.ds(l, 32, stride=16), :] = bufs[t, :, l * LANES : (l + 1) * LANES].astype(
                f32
            )
        rows_ref[:, t * 32 : (t + 1) * 32, :] = scr_ref[t].reshape(16, 32, LANES).astype(bf16)
        for k in range(TURNS):
            for y in range(4):
                tile = ((x + k) & (TURNS - 1)) * 4 + y
                cols = pl.ds(pl.multiple_of(tile * LANES, LANES), LANES)
                a = bufs[t, 0:16, cols].astype(f32)
                b = bufs[t, 16:32, cols].astype(f32)
                first = jnp.where(low, a, pltpu.roll(b, 64, 1))
                second = jnp.where(low, pltpu.roll(a, 64, 1), b)
                cols_refs[k][2 * y, t * 16 : (t + 1) * 16, :] = first.astype(bf16)
                cols_refs[k][2 * y + 1, t * 16 : (t + 1) * 16, :] = second.astype(bf16)
    copies[4].wait()
    keep = e_ref[...].astype(f32).astype(bf16)
    halves = [
        dot((iota((16, 32), 1) == 2 * iota((16, 32), 0) + s).astype(f32).astype(bf16), keep)
        for s in range(2)
    ]
    plane = jnp.concatenate(halves, axis=1)
    for j in range(16):
        rows_ref[j, 128:136, :] = jnp.broadcast_to(plane[j : j + 1, :], (8, LANES)).astype(bf16)
    n = iota((32, 64), 0)
    target = ((x + n // 8) & (TURNS - 1)) * 8 + n % 8
    parts = [
        dot((iota((32, 64), 1) == 2 * target + pp).astype(f32).astype(bf16), keep, 1, 1)
        for pp in range(2)
    ]
    plane = jnp.concatenate(parts + [jnp.zeros((32, 64), f32)], axis=1)
    for n in range(32):
        cols_refs[n // 8][n % 8, 64:72, :] = jnp.broadcast_to(
            plane[n : n + 1, :], (8, LANES)
        ).astype(bf16)


def attend_body(rows, x_ref, in_ref, out_ref, qx, gx, gt, kx, kt, vx, vt, dqt, dk, dv, st, da, wl):
    peers = 16 if rows else 32
    items = 2 if rows else 1
    group = 256 if rows else 512
    turns = 4 if rows else 2
    turn = LANES // turns
    tensor_rows = 32 if rows else 16
    plane = in_ref[:, 4 * tensor_rows, :]
    lane = iota((group, LANES), 1)
    sub = iota((group, LANES), 0) % 16
    for item in range(items):
        parts = []
        for t in range(4):
            first = t * tensor_rows + item * 16
            parts.append(in_ref[:, first : first + 16, :].reshape(group, LANES).astype(f32))
        q4, k4, v4, g4 = parts
        spread = (iota((group, peers), 0) // 16 == iota((group, peers), 1)).astype(f32).astype(bf16)
        barred = 1.0 - dot(spread, plane)
        src, dst = iota((LANES, LANES), 0), iota((LANES, LANES), 1)
        if rows:
            here = lane // 4 == item * 16 + sub
            place = dst == CH * (src % 4)
        else:
            here = (lane % 16 == sub) & (lane < 64)
            place = dst == 64 * ((src // 16) % 2) + 32 * (src // 32)
        mark = jnp.where(here, barred, 0.0).astype(bf16)
        bias = dot(mark, place.astype(f32).astype(bf16)) * masked_score
        kt4, vt4, gt4 = k4.T, v4.T, g4.T
        for d in range(turns):
            span = slice(d * group, (d + 1) * group)

            def turned(x):
                return pltpu.roll(x, turn * d, 1) if d else x

            kx[item, span, 0:LANES] = turned(k4).astype(bf16)
            kx[item, span, LANES : 2 * LANES] = turned(bias).astype(bf16)
            vx[item, span, :] = turned(v4).astype(bf16)
            for a in range(BLOCKS):
                b = (a - d * turn // CH) % BLOCKS
                kt[item, a, :, span] = kt4[b * CH : (b + 1) * CH, :].astype(bf16)
                vt[item, a, :, span] = vt4[b * CH : (b + 1) * CH, :].astype(bf16)
        for a in range(BLOCKS):
            mine = lane // CH == a
            qa = jnp.where(mine, q4, 0.0).astype(bf16)
            ga = jnp.where(mine, g4, 0.0).astype(bf16)
            pick = (iota((QB, LANES), 1) == a * CH).astype(f32).astype(bf16)
            for part in range(group // QB):
                step = (item + part) * BLOCKS + a
                qx[step, :, 0:LANES] = qa[part * QB : (part + 1) * QB, :]
                qx[step, :, LANES : 2 * LANES] = pick
                gx[step] = ga[part * QB : (part + 1) * QB, :]
                gt[step] = gt4[a * CH : (a + 1) * CH, part * QB : (part + 1) * QB]
    dk[...] = jnp.zeros(dk.shape, f32)
    dv[...] = jnp.zeros(dv.shape, f32)
    chunks = [slice(c * KC, (c + 1) * KC) for c in range(KEYS // KC)]

    def one_step(step, carry):
        item = step // BLOCKS if rows else 0
        block = step % BLOCKS
        q = qx[step]
        g = gx[step]
        top = jnp.full((8, QB), -jnp.inf, f32)
        for c in chunks:
            s = dot(kx[item, c, :], q, 1, 1)
            st[c, :] = s
            top = jnp.maximum(top, jnp.max(s.reshape(KC // 8, 8, QB), axis=0))
            da[c, :] = dot(vx[item, c, :], g, 1, 1)
        top = jnp.max(top, axis=0, keepdims=True)
        total = jnp.zeros((8, QB), f32)
        for c in chunks:
            e = jnp.exp2((st[c, :] - top) * EXP2_SCALE)
            st[c, :] = e
            total += jnp.sum(e.reshape(KC // 8, 8, QB), axis=0)
        inverse = 1.0 / jnp.sum(total, axis=0, keepdims=True)
        out = jnp.zeros((CH, QB), f32)
        for c in chunks:
            w = (st[c, :] * inverse).astype(bf16)
            wl[c, :] = w
            out += dot(vt[item, block, :, c], w)
        delta = jnp.sum(gt[step] * out, axis=0, keepdims=True)
        inverse = inverse * SCALE
        dq = jnp.zeros((CH, QB), f32)
        for c in chunks:
            ds = (st[c, :] * inverse * (da[c, :] - delta)).astype(bf16)
            dv[item, c, :] += dot(wl[c, :], g)
            dk[item, c, :] += dot(ds, q[:, 0:LANES])
            dq += dot(kt[item, block, :, c], ds)
        dqt[step] = dq
        return carry

    lax.fori_loop(0, 8, one_step, 0)

    for item in range(items):
        dq4 = [
            dqt[(item + part) * BLOCKS : (item + part + 1) * BLOCKS].reshape(LANES, QB).T
            for part in range(group // QB)
        ]
        sums = [jnp.concatenate(dq4, axis=0) if len(dq4) > 1 else dq4[0]]
        for acc in (dk, dv):
            total = acc[item, 0:group, :]
            for d in range(1, turns):
                total += pltpu.roll(acc[item, d * group : (d + 1) * group, :], LANES - turn * d, 1)
            sums.append(total)
        for t in range(3):
            first = t * tensor_rows + item * 16
            block = sums[t].reshape(peers, 16, LANES).astype(bf16)
            if rows:
                out_ref[:, first : first + 16, :] = block
                continue
            for n in range(peers):
                source = ((x_ref[0] + TURNS - n % TURNS) & (TURNS - 1)) * 8 + n // TURNS
                out_ref[source, first : first + 16, :] = block[n]


def attend(rows, x, received):
    items = 2 if rows else 1
    peers = 16 if rows else 32
    scratch = [
        pltpu.VMEM((8, QB, 2 * LANES), bf16),
        pltpu.VMEM((8, QB, LANES), bf16),
        pltpu.VMEM((8, CH, QB), f32),
        pltpu.VMEM((items, KEYS, 2 * LANES), bf16),
        pltpu.VMEM((items, BLOCKS, CH, KEYS), bf16),
        pltpu.VMEM((items, KEYS, LANES), bf16),
        pltpu.VMEM((items, BLOCKS, CH, KEYS), bf16),
        pltpu.VMEM((8, CH, QB), f32),
        pltpu.VMEM((items, KEYS, LANES), f32),
        pltpu.VMEM((items, KEYS, LANES), f32),
        pltpu.VMEM((KEYS, QB), f32),
        pltpu.VMEM((KEYS, QB), f32),
        pltpu.VMEM((KEYS, QB), bf16),
    ]
    out = jax.ShapeDtypeStruct((peers, 96 if rows else 48, LANES), bf16)
    spaces = [pltpu.SMEM, pltpu.VMEM]
    return call(functools.partial(attend_body, rows), out, scratch, x, received, spaces=spaces)


def unpack_rows_body(in_ref, out_ref, scr_ref):
    for t in range(3):
        scr_ref[t] = in_ref[:, t * 32 : (t + 1) * 32, :].reshape(512, LANES).astype(f32)
    for t in range(3):
        for l in range(16):
            out_ref[t, :, l * LANES : (l + 1) * LANES] = scr_ref[t, pl.ds(l, 32, stride=16), :]


def finish_body(rows_ref, in_ref, q_ref, k_ref, v_ref):
    low = iota((16, LANES), 1) < 64
    for t, ref in enumerate((q_ref, k_ref, v_ref)):
        for l in range(16):
            cols = slice(l * LANES, (l + 1) * LANES)
            a = in_ref[2 * l, t * 16 : (t + 1) * 16, :].astype(f32)
            b = in_ref[2 * l + 1, t * 16 : (t + 1) * 16, :].astype(f32)
            ref[0:16, cols] = rows_ref[t, 0:16, cols] + jnp.where(low, a, pltpu.roll(b, 64, 1))
            ref[16:32, cols] = rows_ref[t, 16:32, cols] + jnp.where(low, pltpu.roll(a, 64, 1), b)


def exchange(array, axis, groups=None):
    return lax.all_to_all(
        array, axis, split_axis=0, concat_axis=0, tiled=True, axis_index_groups=groups
    )


def pack(x, *args):
    outs = [jax.ShapeDtypeStruct((16, 136, LANES), bf16)]
    outs += [jax.ShapeDtypeStruct((8, 72, LANES), bf16)] * TURNS
    scratch = [
        pltpu.VMEM((4, 32, 2048), bf16),
        pltpu.VMEM((32, 64), jnp.int32),
        pltpu.VMEM((4, 512, LANES), f32),
        pltpu.SemaphoreType.DMA((5,)),
    ]
    spaces = [pltpu.SMEM] + [pltpu.HBM] * 5
    args = [pltpu.with_memory_space_constraint(a, pltpu.HBM) for a in args]
    return call(pack_body, outs, scratch, x, *args, spaces=spaces)


def unpack_rows(array):
    out = jax.ShapeDtypeStruct((3, 32, 2048), f32)
    return call(unpack_rows_body, out, [pltpu.VMEM((3, 512, LANES), f32)], array)


def finish(row_part, array):
    return call(finish_body, [jax.ShapeDtypeStruct((32, 2048), f32)] * 3, [], row_part, array)


def per_device(*args):
    x = (lax.axis_index("res") >> 3).reshape(1)
    row_send, *col_send = pack(x, *args)
    row_in = exchange(row_send, "prog")
    turned = [col_send[0]]
    for k in range(1, TURNS):
        turns = [(i, (i + 8 * k) % 32) for i in range(32)]
        turned.append(lax.ppermute(col_send[k], "res", turns))
    planes = [[8 * i + w for w in range(8)] for i in range(TURNS)]
    col_in = exchange(jnp.stack(turned, axis=1).reshape(8, 288, LANES), "res", planes)
    row_out = exchange(attend(True, x, row_in), "prog")
    col_out = exchange(attend(False, x, col_in.reshape(32, 72, LANES)), "res")
    return tuple(finish(unpack_rows(row_out), col_out))


def solution(mesh):
    return jax.shard_map(
        per_device,
        mesh=mesh,
        in_specs=(P("res", "prog"),) * 5,
        out_specs=(P("res", "prog"),) * 3,
        check_vma=False,
    )
```

```python
import functools
import math

import jax
import jax.numpy as jnp
from jax import lax
from jax.experimental import pallas as pl
from jax.experimental.pallas import tpu as pltpu
from jax.sharding import PartitionSpec as P

CH = 32
LANES = 128
BLOCKS = LANES // CH
SCALE = 1.0 / math.sqrt(CH)
EXP2_SCALE = SCALE * math.log2(math.e)
masked_score = -1e30
INTERPRET = False
QB = 256
KEYS = 1024
KC = 256
TURNS = 4

f32 = jnp.float32
bf16 = jnp.bfloat16


def iota(shape, dim):
    return lax.broadcasted_iota(jnp.int32, shape, dim)


def dot(x, y, cx=1, cy=0):
    return lax.dot_general(x, y, (((cx,), (cy,)), ((), ())), preferred_element_type=f32)


def call(body, outs, scratch, *args, spaces=None):
    return pl.pallas_call(
        body,
        out_shape=outs,
        in_specs=[pl.BlockSpec(memory_space=m) for m in spaces or [pltpu.VMEM] * len(args)],
        out_specs=jax.tree.map(lambda _: pl.BlockSpec(memory_space=pltpu.VMEM), outs),
        scratch_shapes=scratch,
        interpret=INTERPRET,
        compiler_params=pltpu.CompilerParams(vmem_limit_bytes=48 * 2**20),
    )(*args)


def pack_body(x_ref, *refs):
    hbm, e_hbm, rows_ref, cols_refs = refs[:4], refs[4], refs[5], refs[6:10]
    bufs, e_ref, scr_ref, sems = refs[10:]
    copies = [pltpu.make_async_copy(hbm[t], bufs.at[t], sems.at[t]) for t in range(4)]
    copies.append(pltpu.make_async_copy(e_hbm, e_ref, sems.at[4]))
    for copy in copies:
        copy.start()
    x = x_ref[0]
    low = iota((16, LANES), 1) < 64
    for t in range(4):
        copies[t].wait()
        for l in range(16):
            scr_ref[t, pl.ds(l, 32, stride=16), :] = bufs[t, :, l * LANES : (l + 1) * LANES].astype(
                f32
            )
        rows_ref[:, t * 32 : (t + 1) * 32, :] = scr_ref[t].reshape(16, 32, LANES).astype(bf16)
        for k in range(TURNS):
            for y in range(4):
                tile = ((x + k) & (TURNS - 1)) * 4 + y
                cols = pl.ds(pl.multiple_of(tile * LANES, LANES), LANES)
                a = bufs[t, 0:16, cols].astype(f32)
                b = bufs[t, 16:32, cols].astype(f32)
                first = jnp.where(low, a, pltpu.roll(b, 64, 1))
                second = jnp.where(low, pltpu.roll(a, 64, 1), b)
                cols_refs[k][2 * y, t * 16 : (t + 1) * 16, :] = first.astype(bf16)
                cols_refs[k][2 * y + 1, t * 16 : (t + 1) * 16, :] = second.astype(bf16)
    copies[4].wait()
    keep = e_ref[...].astype(f32).astype(bf16)
    halves = [
        dot((iota((16, 32), 1) == 2 * iota((16, 32), 0) + s).astype(f32).astype(bf16), keep)
        for s in range(2)
    ]
    plane = jnp.concatenate(halves, axis=1)
    for j in range(16):
        rows_ref[j, 128:136, :] = jnp.broadcast_to(plane[j : j + 1, :], (8, LANES)).astype(bf16)
    n = iota((32, 64), 0)
    target = ((x + n // 8) & (TURNS - 1)) * 8 + n % 8
    parts = [
        dot((iota((32, 64), 1) == 2 * target + pp).astype(f32).astype(bf16), keep, 1, 1)
        for pp in range(2)
    ]
    plane = jnp.concatenate(parts + [jnp.zeros((32, 64), f32)], axis=1)
    for n in range(32):
        cols_refs[n // 8][n % 8, 64:72, :] = jnp.broadcast_to(
            plane[n : n + 1, :], (8, LANES)
        ).astype(bf16)


def attend_body(rows, x_ref, in_ref, out_ref, qx, gx, gt, kx, kt, vx, vt, dqt, dk, dv, st, da, st2, da2, wl):
    peers = 16 if rows else 32
    items = 2 if rows else 1
    group = 256 if rows else 512
    turns = 4 if rows else 2
    turn = LANES // turns
    tensor_rows = 32 if rows else 16
    if rows:
        plane = in_ref[:, 4 * tensor_rows, :]
    else:
        planes = [in_ref[:, 256 + 2 * k, :].astype(f32) for k in range(TURNS)]
        plane = jnp.stack(planes, axis=1).reshape(peers, LANES).astype(bf16)
    lane = iota((group, LANES), 1)
    sub = iota((group, LANES), 0) % 16
    for item in range(items):
        parts = []
        for t in range(4):
            first = t * tensor_rows + item * 16
            if rows:
                part = in_ref[:, first : first + 16, :]
            else:
                turned = [in_ref[:, k * 64 + first : k * 64 + first + 16, :] for k in range(TURNS)]
                part = jnp.stack(turned, axis=1)
            parts.append(part.reshape(group, LANES).astype(f32))
        q4, k4, v4, g4 = parts
        spread = (iota((group, peers), 0) // 16 == iota((group, peers), 1)).astype(f32).astype(bf16)
        barred = 1.0 - dot(spread, plane)
        src, dst = iota((LANES, LANES), 0), iota((LANES, LANES), 1)
        if rows:
            here = lane // 4 == item * 16 + sub
            place = dst == CH * (src % 4)
        else:
            here = (lane % 16 == sub) & (lane < 64)
            place = dst == 64 * ((src // 16) % 2) + 32 * (src // 32)
        mark = jnp.where(here, barred, 0.0).astype(bf16)
        bias = dot(mark, place.astype(f32).astype(bf16)) * masked_score
        kt4, vt4, gt4 = k4.T, v4.T, g4.T
        for d in range(turns):
            span = slice(d * group, (d + 1) * group)

            def turned(x):
                return pltpu.roll(x, turn * d, 1) if d else x

            kx[item, span, 0:LANES] = turned(k4).astype(bf16)
            kx[item, span, LANES : 2 * LANES] = turned(bias).astype(bf16)
            vx[item, span, :] = turned(v4).astype(bf16)
            for a in range(BLOCKS):
                b = (a - d * turn // CH) % BLOCKS
                kt[item, a, :, span] = kt4[b * CH : (b + 1) * CH, :].astype(bf16)
                vt[item, a, :, span] = vt4[b * CH : (b + 1) * CH, :].astype(bf16)
        for a in range(BLOCKS):
            mine = lane // CH == a
            qa = jnp.where(mine, q4, 0.0).astype(bf16)
            ga = jnp.where(mine, g4, 0.0).astype(bf16)
            pick = (iota((QB, LANES), 1) == a * CH).astype(f32).astype(bf16)
            for part in range(group // QB):
                step = (item + part) * BLOCKS + a
                qx[step, :, 0:LANES] = qa[part * QB : (part + 1) * QB, :]
                qx[step, :, LANES : 2 * LANES] = pick
                gx[step] = ga[part * QB : (part + 1) * QB, :]
                gt[step] = gt4[a * CH : (a + 1) * CH, part * QB : (part + 1) * QB]
    dk[...] = jnp.zeros(dk.shape, f32)
    dv[...] = jnp.zeros(dv.shape, f32)
    chunks = [slice(c * KC, (c + 1) * KC) for c in range(KEYS // KC)]

    def item_of(step):
        return step // BLOCKS if rows else 0

    def score_chunk(step, bufs, c, top):
        s = dot(kx[item_of(step), c, :], qx[step], 1, 1)
        bufs[0][c, :] = s
        return jnp.maximum(top, jnp.max(s.reshape(KC // 8, 8, QB), axis=0))

    def expo_chunk(step, bufs, c, top, total):
        bufs[1][c, :] = dot(vx[item_of(step), c, :], gx[step], 1, 1)
        e = jnp.exp2((bufs[0][c, :] - top) * EXP2_SCALE)
        bufs[0][c, :] = e
        return total + jnp.sum(e.reshape(KC // 8, 8, QB), axis=0)

    def weight_chunk(step, bufs, c, inverse, out):
        w = (bufs[0][c, :] * inverse).astype(bf16)
        wl[c, :] = w
        return out + dot(vt[item_of(step), step % BLOCKS, :, c], w)

    def grad_chunk(step, bufs, c, inverse, delta, dq):
        item = item_of(step)
        ds = (bufs[0][c, :] * inverse * (bufs[1][c, :] - delta)).astype(bf16)
        dv[item, c, :] += dot(wl[c, :], gx[step])
        dk[item, c, :] += dot(ds, qx[step, :, 0:LANES])
        return dq + dot(kt[item, step % BLOCKS, :, c], ds)

    def fused(step, bufs, inverse, after, after_bufs):
        top = jnp.full((8, QB), -jnp.inf, f32)
        out = jnp.zeros((CH, QB), f32)
        for c in chunks:
            if after is not None:
                top = score_chunk(after, after_bufs, c, top)
            if step is not None:
                out = weight_chunk(step, bufs, c, inverse, out)
        top = jnp.max(top, axis=0, keepdims=True)
        if step is not None:
            delta = jnp.sum(gt[step] * out, axis=0, keepdims=True)
            scaled = inverse * SCALE
        total = jnp.zeros((8, QB), f32)
        dq = jnp.zeros((CH, QB), f32)
        for c in chunks:
            if step is not None:
                dq = grad_chunk(step, bufs, c, scaled, delta, dq)
            if after is not None:
                total = expo_chunk(after, after_bufs, c, top, total)
        if step is not None:
            dqt[step] = dq
        return 1.0 / jnp.sum(total, axis=0, keepdims=True)

    even, odd = (st, da), (st2, da2)

    def two_steps(pair, inverse):
        inverse = fused(2 * pair, even, inverse, 2 * pair + 1, odd)
        return fused(2 * pair + 1, odd, inverse, 2 * pair + 2, even)

    inverse = fused(None, None, None, 0, even)
    inverse = lax.fori_loop(0, 3, two_steps, inverse)
    inverse = fused(6, even, inverse, 7, odd)
    fused(7, odd, inverse, None, None)

    for item in range(items):
        dq4 = [
            dqt[(item + part) * BLOCKS : (item + part + 1) * BLOCKS].reshape(LANES, QB).T
            for part in range(group // QB)
        ]
        sums = [jnp.concatenate(dq4, axis=0) if len(dq4) > 1 else dq4[0]]
        for acc in (dk, dv):
            total = acc[item, 0:group, :]
            for d in range(1, turns):
                total += pltpu.roll(acc[item, d * group : (d + 1) * group, :], LANES - turn * d, 1)
            sums.append(total)
        for t in range(3):
            first = t * tensor_rows + item * 16
            block = sums[t].reshape(peers, 16, LANES).astype(bf16)
            if rows:
                out_ref[:, first : first + 16, :] = block
                continue
            for n in range(peers):
                source = ((x_ref[0] + TURNS - n % TURNS) & (TURNS - 1)) * 8 + n // TURNS
                out_ref[source, first : first + 16, :] = block[n]


def attend(rows, x, received):
    items = 2 if rows else 1
    peers = 16 if rows else 32
    scratch = [
        pltpu.VMEM((8, QB, 2 * LANES), bf16),
        pltpu.VMEM((8, QB, LANES), bf16),
        pltpu.VMEM((8, CH, QB), f32),
        pltpu.VMEM((items, KEYS, 2 * LANES), bf16),
        pltpu.VMEM((items, BLOCKS, CH, KEYS), bf16),
        pltpu.VMEM((items, KEYS, LANES), bf16),
        pltpu.VMEM((items, BLOCKS, CH, KEYS), bf16),
        pltpu.VMEM((8, CH, QB), f32),
        pltpu.VMEM((items, KEYS, LANES), f32),
        pltpu.VMEM((items, KEYS, LANES), f32),
        pltpu.VMEM((KEYS, QB), f32),
        pltpu.VMEM((KEYS, QB), f32),
        pltpu.VMEM((KEYS, QB), f32),
        pltpu.VMEM((KEYS, QB), f32),
        pltpu.VMEM((KEYS, QB), bf16),
    ]
    out = jax.ShapeDtypeStruct((peers, 96 if rows else 48, LANES), bf16)
    spaces = [pltpu.SMEM, pltpu.VMEM]
    return call(functools.partial(attend_body, rows), out, scratch, x, received, spaces=spaces)


def regroup_body(*refs):
    out_ref = refs[TURNS]
    row = iota((8, LANES), 0) // 2
    for w in range(8):
        tile = jnp.zeros((8, LANES), f32)
        for k in range(TURNS):
            out_ref[w, k * 64 : (k + 1) * 64, :] = refs[k][w, 0:64, :]
            tile = jnp.where(row == k, refs[k][w, 64:72, :].astype(f32), tile)
        out_ref[w, 256:264, :] = tile.astype(bf16)


def unpack_rows_body(in_ref, out_ref, scr_ref):
    for t in range(3):
        scr_ref[t] = in_ref[:, t * 32 : (t + 1) * 32, :].reshape(512, LANES).astype(f32)
    for t in range(3):
        for l in range(16):
            out_ref[t, :, l * LANES : (l + 1) * LANES] = scr_ref[t, pl.ds(l, 32, stride=16), :]


def finish_body(rows_ref, in_ref, q_ref, k_ref, v_ref):
    low = iota((16, LANES), 1) < 64
    for t, ref in enumerate((q_ref, k_ref, v_ref)):
        for l in range(16):
            cols = slice(l * LANES, (l + 1) * LANES)
            a = in_ref[2 * l, t * 16 : (t + 1) * 16, :].astype(f32)
            b = in_ref[2 * l + 1, t * 16 : (t + 1) * 16, :].astype(f32)
            ref[0:16, cols] = rows_ref[t, 0:16, cols] + jnp.where(low, a, pltpu.roll(b, 64, 1))
            ref[16:32, cols] = rows_ref[t, 16:32, cols] + jnp.where(low, pltpu.roll(a, 64, 1), b)


def exchange(array, axis, groups=None):
    return lax.all_to_all(
        array, axis, split_axis=0, concat_axis=0, tiled=True, axis_index_groups=groups
    )


def pack(x, *args):
    outs = [jax.ShapeDtypeStruct((16, 136, LANES), bf16)]
    outs += [jax.ShapeDtypeStruct((8, 72, LANES), bf16)] * TURNS
    scratch = [
        pltpu.VMEM((4, 32, 2048), bf16),
        pltpu.VMEM((32, 64), jnp.int32),
        pltpu.VMEM((4, 512, LANES), f32),
        pltpu.SemaphoreType.DMA((5,)),
    ]
    spaces = [pltpu.SMEM] + [pltpu.HBM] * 5
    args = [pltpu.with_memory_space_constraint(a, pltpu.HBM) for a in args]
    return call(pack_body, outs, scratch, x, *args, spaces=spaces)


def regroup(arrays):
    return call(regroup_body, jax.ShapeDtypeStruct((8, 264, LANES), bf16), [], *arrays)


def unpack_rows(array):
    out = jax.ShapeDtypeStruct((3, 32, 2048), f32)
    return call(unpack_rows_body, out, [pltpu.VMEM((3, 512, LANES), f32)], array)


def finish(row_part, array):
    return call(finish_body, [jax.ShapeDtypeStruct((32, 2048), f32)] * 3, [], row_part, array)


def per_device(*args):
    x = (lax.axis_index("res") >> 3).reshape(1)
    row_send, *col_send = pack(x, *args)
    row_in = exchange(row_send, "prog")
    turned = [col_send[0]]
    for k in range(1, TURNS):
        turns = [(i, (i + 8 * k) % 32) for i in range(32)]
        turned.append(lax.ppermute(col_send[k], "res", turns))
    planes = [[8 * i + w for w in range(8)] for i in range(TURNS)]
    col_in = exchange(regroup(turned), "res", planes)
    row_out = exchange(attend(True, x, row_in), "prog")
    col_out = exchange(attend(False, x, col_in), "res")
    return tuple(finish(unpack_rows(row_out), col_out))


def solution(mesh):
    return jax.shard_map(
        per_device,
        mesh=mesh,
        in_specs=(P("res", "prog"),) * 5,
        out_specs=(P("res", "prog"),) * 3,
        check_vma=False,
    )
```

```python
import functools
import math

import jax
import jax.numpy as jnp
from jax import lax
from jax.experimental import pallas as pl
from jax.experimental.pallas import tpu as pltpu
from jax.sharding import PartitionSpec as P

CH = 32
LANES = 128
BLOCKS = LANES // CH
SCALE = 1.0 / math.sqrt(CH)
EXP2_SCALE = SCALE * math.log2(math.e)
masked_score = -1e30
INTERPRET = False
QB = 256
KEYS = 1024
KC = 256
TURNS = 4

f32 = jnp.float32
bf16 = jnp.bfloat16


def iota(shape, dim):
    return lax.broadcasted_iota(jnp.int32, shape, dim)


def dot(x, y, cx=1, cy=0):
    return lax.dot_general(x, y, (((cx,), (cy,)), ((), ())), preferred_element_type=f32)


def call(body, outs, scratch, *args, spaces=None, out_spaces=None):
    return pl.pallas_call(
        body,
        out_shape=outs,
        in_specs=[pl.BlockSpec(memory_space=m) for m in spaces or [pltpu.VMEM] * len(args)],
        out_specs=out_spaces or jax.tree.map(lambda _: pl.BlockSpec(memory_space=pltpu.VMEM), outs),
        scratch_shapes=scratch,
        interpret=INTERPRET,
        compiler_params=pltpu.CompilerParams(vmem_limit_bytes=48 * 2**20),
    )(*args)


def pack_body(x_ref, *refs):
    hbm, e_hbm, rows_hbm, cols_refs = refs[:4], refs[4], refs[5], refs[6:10]
    bufs, e_ref, scr_ref, rows_buf, plane_buf, sems, out_sems = refs[10:]
    copies = [pltpu.make_async_copy(hbm[t], bufs.at[t], sems.at[t]) for t in range(4)]
    copies.append(pltpu.make_async_copy(e_hbm, e_ref, sems.at[4]))
    for copy in copies:
        copy.start()
    sends = [
        pltpu.make_async_copy(
            rows_buf.at[t], rows_hbm.at[:, t * 32 : (t + 1) * 32, :], out_sems.at[t]
        )
        for t in range(4)
    ]
    sends.append(pltpu.make_async_copy(plane_buf, rows_hbm.at[:, 128:136, :], out_sems.at[4]))
    x = x_ref[0]
    low = iota((16, LANES), 1) < 64
    for t in range(4):
        copies[t].wait()
        for l in range(16):
            scr_ref[t, pl.ds(l, 32, stride=16), :] = bufs[t, :, l * LANES : (l + 1) * LANES].astype(
                f32
            )
        rows_buf[t] = scr_ref[t].reshape(16, 32, LANES).astype(bf16)
        sends[t].start()
    copies[4].wait()
    keep = e_ref[...].astype(f32).astype(bf16)
    halves = [
        dot((iota((16, 32), 1) == 2 * iota((16, 32), 0) + s).astype(f32).astype(bf16), keep)
        for s in range(2)
    ]
    plane = jnp.concatenate(halves, axis=1)
    for j in range(16):
        plane_buf[j] = jnp.broadcast_to(plane[j : j + 1, :], (8, LANES)).astype(bf16)
    sends[4].start()
    for t in range(4):
        for k in range(TURNS):
            for y in range(4):
                tile = ((x + k) & (TURNS - 1)) * 4 + y
                cols = pl.ds(pl.multiple_of(tile * LANES, LANES), LANES)
                a = bufs[t, 0:16, cols].astype(f32)
                b = bufs[t, 16:32, cols].astype(f32)
                first = jnp.where(low, a, pltpu.roll(b, 64, 1))
                second = jnp.where(low, pltpu.roll(a, 64, 1), b)
                cols_refs[k][2 * y, t * 16 : (t + 1) * 16, :] = first.astype(bf16)
                cols_refs[k][2 * y + 1, t * 16 : (t + 1) * 16, :] = second.astype(bf16)
    n = iota((32, 64), 0)
    target = ((x + n // 8) & (TURNS - 1)) * 8 + n % 8
    parts = [
        dot((iota((32, 64), 1) == 2 * target + pp).astype(f32).astype(bf16), keep, 1, 1)
        for pp in range(2)
    ]
    plane = jnp.concatenate(parts + [jnp.zeros((32, 64), f32)], axis=1)
    for n in range(32):
        cols_refs[n // 8][n % 8, 64:72, :] = jnp.broadcast_to(
            plane[n : n + 1, :], (8, LANES)
        ).astype(bf16)
    for send in sends:
        send.wait()


def attend_body(rows, x_ref, in_ref, out_ref, qx, gx, gt, kx, kt, vx, vt, dqt, dk, dv, st, da, st2, da2, wl):
    peers = 16 if rows else 32
    items = 2 if rows else 1
    group = 256 if rows else 512
    turns = 4 if rows else 2
    turn = LANES // turns
    tensor_rows = 32 if rows else 16
    if rows:
        plane = in_ref[:, 4 * tensor_rows, :]
    else:
        planes = [in_ref[:, 256 + 2 * k, :].astype(f32) for k in range(TURNS)]
        plane = jnp.stack(planes, axis=1).reshape(peers, LANES).astype(bf16)
    lane = iota((group, LANES), 1)
    sub = iota((group, LANES), 0) % 16
    for item in range(items):
        parts = []
        for t in range(4):
            first = t * tensor_rows + item * 16
            if rows:
                part = in_ref[:, first : first + 16, :]
            else:
                turned = [in_ref[:, k * 64 + first : k * 64 + first + 16, :] for k in range(TURNS)]
                part = jnp.stack(turned, axis=1)
            parts.append(part.reshape(group, LANES).astype(f32))
        q4, k4, v4, g4 = parts
        spread = (iota((group, peers), 0) // 16 == iota((group, peers), 1)).astype(f32).astype(bf16)
        barred = 1.0 - dot(spread, plane)
        src, dst = iota((LANES, LANES), 0), iota((LANES, LANES), 1)
        if rows:
            here = lane // 4 == item * 16 + sub
            place = dst == CH * (src % 4)
        else:
            here = (lane % 16 == sub) & (lane < 64)
            place = dst == 64 * ((src // 16) % 2) + 32 * (src // 32)
        mark = jnp.where(here, barred, 0.0).astype(bf16)
        bias = dot(mark, place.astype(f32).astype(bf16)) * masked_score
        kt4, vt4, gt4 = k4.T, v4.T, g4.T
        for d in range(turns):
            span = slice(d * group, (d + 1) * group)

            def turned(x):
                return pltpu.roll(x, turn * d, 1) if d else x

            kx[item, span, 0:LANES] = turned(k4).astype(bf16)
            kx[item, span, LANES : 2 * LANES] = turned(bias).astype(bf16)
            vx[item, span, :] = turned(v4).astype(bf16)
            for a in range(BLOCKS):
                b = (a - d * turn // CH) % BLOCKS
                kt[item, a, :, span] = kt4[b * CH : (b + 1) * CH, :].astype(bf16)
                vt[item, a, :, span] = vt4[b * CH : (b + 1) * CH, :].astype(bf16)
        for a in range(BLOCKS):
            mine = lane // CH == a
            qa = jnp.where(mine, q4, 0.0).astype(bf16)
            ga = jnp.where(mine, g4, 0.0).astype(bf16)
            pick = (iota((QB, LANES), 1) == a * CH).astype(f32).astype(bf16)
            for part in range(group // QB):
                step = (item + part) * BLOCKS + a
                qx[step, :, 0:LANES] = qa[part * QB : (part + 1) * QB, :]
                qx[step, :, LANES : 2 * LANES] = pick
                gx[step] = ga[part * QB : (part + 1) * QB, :]
                gt[step] = gt4[a * CH : (a + 1) * CH, part * QB : (part + 1) * QB]
    dk[...] = jnp.zeros(dk.shape, f32)
    dv[...] = jnp.zeros(dv.shape, f32)
    chunks = [slice(c * KC, (c + 1) * KC) for c in range(KEYS // KC)]

    def item_of(step):
        return step // BLOCKS if rows else 0

    def score_chunk(step, bufs, c, top):
        s = dot(kx[item_of(step), c, :], qx[step], 1, 1)
        bufs[0][c, :] = s
        return jnp.maximum(top, jnp.max(s.reshape(KC // 8, 8, QB), axis=0))

    def expo_chunk(step, bufs, c, top, total):
        bufs[1][c, :] = dot(vx[item_of(step), c, :], gx[step], 1, 1)
        e = jnp.exp2((bufs[0][c, :] - top) * EXP2_SCALE)
        bufs[0][c, :] = e
        return total + jnp.sum(e.reshape(KC // 8, 8, QB), axis=0)

    def weight_chunk(step, bufs, c, inverse, out):
        w = (bufs[0][c, :] * inverse).astype(bf16)
        wl[c, :] = w
        return out + dot(vt[item_of(step), step % BLOCKS, :, c], w)

    def grad_chunk(step, bufs, c, inverse, delta, dq):
        item = item_of(step)
        ds = (bufs[0][c, :] * inverse * (bufs[1][c, :] - delta)).astype(bf16)
        dv[item, c, :] += dot(wl[c, :], gx[step])
        dk[item, c, :] += dot(ds, qx[step, :, 0:LANES])
        return dq + dot(kt[item, step % BLOCKS, :, c], ds)

    def fused(step, bufs, inverse, after, after_bufs):
        top = jnp.full((8, QB), -jnp.inf, f32)
        out = jnp.zeros((CH, QB), f32)
        for c in chunks:
            if after is not None:
                top = score_chunk(after, after_bufs, c, top)
            if step is not None:
                out = weight_chunk(step, bufs, c, inverse, out)
        top = jnp.max(top, axis=0, keepdims=True)
        if step is not None:
            delta = jnp.sum(gt[step] * out, axis=0, keepdims=True)
            scaled = inverse * SCALE
        total = jnp.zeros((8, QB), f32)
        dq = jnp.zeros((CH, QB), f32)
        for c in chunks:
            if step is not None:
                dq = grad_chunk(step, bufs, c, scaled, delta, dq)
            if after is not None:
                total = expo_chunk(after, after_bufs, c, top, total)
        if step is not None:
            dqt[step] = dq
        return 1.0 / jnp.sum(total, axis=0, keepdims=True)

    even, odd = (st, da), (st2, da2)

    def two_steps(pair, inverse):
        inverse = fused(2 * pair, even, inverse, 2 * pair + 1, odd)
        return fused(2 * pair + 1, odd, inverse, 2 * pair + 2, even)

    inverse = fused(None, None, None, 0, even)
    inverse = lax.fori_loop(0, 3, two_steps, inverse)
    inverse = fused(6, even, inverse, 7, odd)
    fused(7, odd, inverse, None, None)

    for item in range(items):
        dq4 = [
            dqt[(item + part) * BLOCKS : (item + part + 1) * BLOCKS].reshape(LANES, QB).T
            for part in range(group // QB)
        ]
        sums = [jnp.concatenate(dq4, axis=0) if len(dq4) > 1 else dq4[0]]
        for acc in (dk, dv):
            total = acc[item, 0:group, :]
            for d in range(1, turns):
                total += pltpu.roll(acc[item, d * group : (d + 1) * group, :], LANES - turn * d, 1)
            sums.append(total)
        for t in range(3):
            first = t * tensor_rows + item * 16
            block = sums[t].reshape(peers, 16, LANES).astype(bf16)
            if rows:
                out_ref[:, first : first + 16, :] = block
                continue
            for n in range(peers):
                source = ((x_ref[0] + TURNS - n % TURNS) & (TURNS - 1)) * 8 + n // TURNS
                out_ref[source, first : first + 16, :] = block[n]


def attend(rows, x, received):
    items = 2 if rows else 1
    peers = 16 if rows else 32
    scratch = [
        pltpu.VMEM((8, QB, 2 * LANES), bf16),
        pltpu.VMEM((8, QB, LANES), bf16),
        pltpu.VMEM((8, CH, QB), f32),
        pltpu.VMEM((items, KEYS, 2 * LANES), bf16),
        pltpu.VMEM((items, BLOCKS, CH, KEYS), bf16),
        pltpu.VMEM((items, KEYS, LANES), bf16),
        pltpu.VMEM((items, BLOCKS, CH, KEYS), bf16),
        pltpu.VMEM((8, CH, QB), f32),
        pltpu.VMEM((items, KEYS, LANES), f32),
        pltpu.VMEM((items, KEYS, LANES), f32),
        pltpu.VMEM((KEYS, QB), f32),
        pltpu.VMEM((KEYS, QB), f32),
        pltpu.VMEM((KEYS, QB), f32),
        pltpu.VMEM((KEYS, QB), f32),
        pltpu.VMEM((KEYS, QB), bf16),
    ]
    out = jax.ShapeDtypeStruct((peers, 96 if rows else 48, LANES), bf16)
    spaces = [pltpu.SMEM, pltpu.VMEM]
    return call(functools.partial(attend_body, rows), out, scratch, x, received, spaces=spaces)


def regroup_body(*refs):
    out_hbm, tile_buf, sems = refs[TURNS:]
    sends = [
        pltpu.make_async_copy(
            refs[k].at[:, 0:64, :], out_hbm.at[:, k * 64 : (k + 1) * 64, :], sems.at[k]
        )
        for k in range(TURNS)
    ]
    sends.append(pltpu.make_async_copy(tile_buf, out_hbm.at[:, 256:264, :], sems.at[TURNS]))
    for send in sends[:TURNS]:
        send.start()
    row = iota((8, LANES), 0) // 2
    for w in range(8):
        tile = jnp.zeros((8, LANES), f32)
        for k in range(TURNS):
            tile = jnp.where(row == k, refs[k][w, 64:72, :].astype(f32), tile)
        tile_buf[w] = tile.astype(bf16)
    sends[TURNS].start()
    for send in sends:
        send.wait()


def unpack_rows_body(in_ref, out_ref, scr_ref):
    for t in range(3):
        scr_ref[t] = in_ref[:, t * 32 : (t + 1) * 32, :].reshape(512, LANES).astype(f32)
    for t in range(3):
        for l in range(16):
            out_ref[t, :, l * LANES : (l + 1) * LANES] = scr_ref[t, pl.ds(l, 32, stride=16), :]


def finish_body(rows_ref, in_ref, q_hbm, k_hbm, v_hbm, bufs, sems):
    low = iota((16, LANES), 1) < 64
    sends = [
        pltpu.make_async_copy(bufs.at[t], hbm, sems.at[t])
        for t, hbm in enumerate((q_hbm, k_hbm, v_hbm))
    ]
    for t in range(3):
        for l in range(16):
            cols = slice(l * LANES, (l + 1) * LANES)
            a = in_ref[2 * l, t * 16 : (t + 1) * 16, :].astype(f32)
            b = in_ref[2 * l + 1, t * 16 : (t + 1) * 16, :].astype(f32)
            upper = jnp.where(low, a, pltpu.roll(b, 64, 1))
            lower = jnp.where(low, pltpu.roll(a, 64, 1), b)
            bufs[t, 0:16, cols] = rows_ref[t, 0:16, cols] + upper
            bufs[t, 16:32, cols] = rows_ref[t, 16:32, cols] + lower
        sends[t].start()
    for send in sends:
        send.wait()


def exchange(array, axis, groups=None):
    return lax.all_to_all(
        array, axis, split_axis=0, concat_axis=0, tiled=True, axis_index_groups=groups
    )


def pack(x, *args):
    outs = [jax.ShapeDtypeStruct((16, 136, LANES), bf16)]
    outs += [jax.ShapeDtypeStruct((8, 72, LANES), bf16)] * TURNS
    scratch = [
        pltpu.VMEM((4, 32, 2048), bf16),
        pltpu.VMEM((32, 64), jnp.int32),
        pltpu.VMEM((4, 512, LANES), f32),
        pltpu.VMEM((4, 16, 32, LANES), bf16),
        pltpu.VMEM((16, 8, LANES), bf16),
        pltpu.SemaphoreType.DMA((5,)),
        pltpu.SemaphoreType.DMA((5,)),
    ]
    spaces = [pltpu.SMEM] + [pltpu.HBM] * 5
    out_spaces = [pl.BlockSpec(memory_space=m) for m in [pltpu.HBM] + [pltpu.VMEM] * TURNS]
    args = [pltpu.with_memory_space_constraint(a, pltpu.HBM) for a in args]
    return call(pack_body, outs, scratch, x, *args, spaces=spaces, out_spaces=out_spaces)


def regroup(arrays):
    scratch = [pltpu.VMEM((8, 8, LANES), bf16), pltpu.SemaphoreType.DMA((TURNS + 1,))]
    out = jax.ShapeDtypeStruct((8, 264, LANES), bf16)
    return call(regroup_body, out, scratch, *arrays, out_spaces=pl.BlockSpec(memory_space=pltpu.HBM))


def unpack_rows(array):
    out = jax.ShapeDtypeStruct((3, 32, 2048), f32)
    return call(unpack_rows_body, out, [pltpu.VMEM((3, 512, LANES), f32)], array)


def finish(row_part, array):
    scratch = [pltpu.VMEM((3, 32, 2048), f32), pltpu.SemaphoreType.DMA((3,))]
    outs = [jax.ShapeDtypeStruct((32, 2048), f32)] * 3
    out_spaces = [pl.BlockSpec(memory_space=pltpu.HBM)] * 3
    return call(finish_body, outs, scratch, row_part, array, out_spaces=out_spaces)


def per_device(*args):
    x = (lax.axis_index("res") >> 3).reshape(1)
    row_send, *col_send = pack(x, *args)
    row_in = exchange(row_send, "prog")
    turned = [col_send[0]]
    for k in range(1, TURNS):
        turns = [(i, (i + 8 * k) % 32) for i in range(32)]
        turned.append(lax.ppermute(col_send[k], "res", turns))
    planes = [[8 * i + w for w in range(8)] for i in range(TURNS)]
    col_in = exchange(regroup(turned), "res", planes)
    row_out = exchange(attend(True, x, row_in), "prog")
    col_out = exchange(attend(False, x, col_in), "res")
    return tuple(finish(unpack_rows(row_out), col_out))


def solution(mesh):
    return jax.shard_map(
        per_device,
        mesh=mesh,
        in_specs=(P("res", "prog"),) * 5,
        out_specs=(P("res", "prog"),) * 3,
        check_vma=False,
    )
```

```python
import functools
import math

import jax
import jax.numpy as jnp
from jax import lax
from jax.experimental import pallas as pl
from jax.experimental.pallas import tpu as pltpu
from jax.sharding import PartitionSpec as P


CH = 32
LANES = 128
BLOCKS = LANES // CH
SCALE = 1.0 / math.sqrt(CH)
EXP2_SCALE = SCALE * math.log2(math.e)
masked_score = -1e30
INTERPRET = False
QB = 256
ORDER = (2, 1, 3)
KEYS = 1024
KC = 256
TURNS = 4

f32 = jnp.float32
bf16 = jnp.bfloat16


def iota(shape, dim):
    return lax.broadcasted_iota(jnp.int32, shape, dim)


def dot(x, y, cx=1, cy=0):
    return lax.dot_general(x, y, (((cx,), (cy,)), ((), ())), preferred_element_type=f32)


def call(body, outs, scratch, *args, spaces=None, out_spaces=None):
    return pl.pallas_call(
        body,
        out_shape=outs,
        in_specs=[pl.BlockSpec(memory_space=m) for m in spaces or [pltpu.VMEM] * len(args)],
        out_specs=out_spaces or jax.tree.map(lambda _: pl.BlockSpec(memory_space=pltpu.VMEM), outs),
        scratch_shapes=scratch,
        interpret=INTERPRET,
        compiler_params=pltpu.CompilerParams(vmem_limit_bytes=48 * 2**20),
    )(*args)


def pack_body(y_ref, *refs):
    hbm, e_hbm, rows_hbm, cols_refs = refs[:4], refs[4], refs[5], refs[6:10]
    bufs, e_ref, scr_ref, rows_buf, plane_buf, sems, out_sems = refs[10:]
    copies = [pltpu.make_async_copy(hbm[t], bufs.at[t], sems.at[t]) for t in range(4)]
    copies.append(pltpu.make_async_copy(e_hbm, e_ref, sems.at[4]))
    for copy in copies:
        copy.start()
    sends = [
        pltpu.make_async_copy(
            rows_buf.at[t], rows_hbm.at[:, t * 32 : (t + 1) * 32, :], out_sems.at[t]
        )
        for t in range(4)
    ]
    sends.append(pltpu.make_async_copy(plane_buf, rows_hbm.at[:, 128:136, :], out_sems.at[4]))
    own_y = y_ref[0]
    low = iota((16, LANES), 1) < 64
    for t in range(4):
        copies[t].wait()
        for l in range(16):
            scr_ref[t, pl.ds(l, 32, stride=16), :] = bufs[t, :, l * LANES : (l + 1) * LANES].astype(
                f32
            )
        rows_buf[t] = scr_ref[t].reshape(16, 32, LANES).astype(bf16)
        sends[t].start()
    copies[4].wait()
    keep = e_ref[...].astype(f32).astype(bf16)
    halves = [
        dot((iota((16, 32), 1) == 2 * iota((16, 32), 0) + s).astype(f32).astype(bf16), keep)
        for s in range(2)
    ]
    plane = jnp.concatenate(halves, axis=1)
    for j in range(16):
        plane_buf[j] = jnp.broadcast_to(plane[j : j + 1, :], (8, LANES)).astype(bf16)
    sends[4].start()
    for t in range(4):
        for k in range(TURNS):
            for x in range(4):
                tile = x * 4 + ((own_y + k) & (TURNS - 1))
                cols = pl.ds(pl.multiple_of(tile * LANES, LANES), LANES)
                a = bufs[t, 0:16, cols].astype(f32)
                b = bufs[t, 16:32, cols].astype(f32)
                first = jnp.where(low, a, pltpu.roll(b, 64, 1))
                second = jnp.where(low, pltpu.roll(a, 64, 1), b)
                cols_refs[k][2 * x, t * 16 : (t + 1) * 16, :] = first.astype(bf16)
                cols_refs[k][2 * x + 1, t * 16 : (t + 1) * 16, :] = second.astype(bf16)
    n = iota((32, 64), 0)
    target = (n % 8) // 2 * 8 + ((own_y + n // 8) & (TURNS - 1)) * 2 + n % 2
    parts = [
        dot((iota((32, 64), 1) == 2 * target + pp).astype(f32).astype(bf16), keep, 1, 1)
        for pp in range(2)
    ]
    plane = jnp.concatenate(parts + [jnp.zeros((32, 64), f32)], axis=1)
    for n in range(32):
        cols_refs[n // 8][n % 8, 64:72, :] = jnp.broadcast_to(
            plane[n : n + 1, :], (8, LANES)
        ).astype(bf16)
    for send in sends:
        send.wait()


def attend_body(rows, y_ref, in_ref, out_ref, qx, gx, gt, kx, kt, vx, vt, dqt, dk, dv, st, da, st2, da2, wl):
    peers = 16 if rows else 32
    items = 2 if rows else 1
    group = 256 if rows else 512
    turns = 4 if rows else 2
    turn = LANES // turns
    tensor_rows = 32 if rows else 16
    if rows:
        plane = in_ref[:, 4 * tensor_rows, :]
    else:
        planes = [in_ref[:, 256 + 2 * k, :].astype(f32) for k in range(TURNS)]
        plane = jnp.stack(planes, axis=1).reshape(peers, LANES).astype(bf16)
    lane = iota((group, LANES), 1)
    sub = iota((group, LANES), 0) % 16
    for item in range(items):
        parts = []
        for t in range(4):
            first = t * tensor_rows + item * 16
            if rows:
                part = in_ref[:, first : first + 16, :]
            else:
                turned = [in_ref[:, k * 64 + first : k * 64 + first + 16, :] for k in range(TURNS)]
                part = jnp.stack(turned, axis=1)
            parts.append(part.reshape(group, LANES).astype(f32))
        q4, k4, v4, g4 = parts
        spread = (iota((group, peers), 0) // 16 == iota((group, peers), 1)).astype(f32).astype(bf16)
        barred = 1.0 - dot(spread, plane)
        src, dst = iota((LANES, LANES), 0), iota((LANES, LANES), 1)
        if rows:
            here = lane // 4 == item * 16 + sub
            place = dst == CH * (src % 4)
        else:
            here = (lane % 16 == sub) & (lane < 64)
            place = dst == 64 * ((src // 16) % 2) + 32 * (src // 32)
        mark = jnp.where(here, barred, 0.0).astype(bf16)
        bias = dot(mark, place.astype(f32).astype(bf16)) * masked_score
        kt4, vt4, gt4 = k4.T, v4.T, g4.T
        for d in range(turns):
            span = slice(d * group, (d + 1) * group)

            def turned(x):
                return pltpu.roll(x, turn * d, 1) if d else x

            kx[item, span, 0:LANES] = turned(k4).astype(bf16)
            kx[item, span, LANES : 2 * LANES] = turned(bias).astype(bf16)
            vx[item, span, :] = turned(v4).astype(bf16)
            for a in range(BLOCKS):
                b = (a - d * turn // CH) % BLOCKS
                kt[item, a, :, span] = kt4[b * CH : (b + 1) * CH, :].astype(bf16)
                vt[item, a, :, span] = vt4[b * CH : (b + 1) * CH, :].astype(bf16)
        for a in range(BLOCKS):
            mine = lane // CH == a
            qa = jnp.where(mine, q4, 0.0).astype(bf16)
            ga = jnp.where(mine, g4, 0.0).astype(bf16)
            pick = (iota((QB, LANES), 1) == a * CH).astype(f32).astype(bf16)
            for part in range(group // QB):
                step = (item + part) * BLOCKS + a
                qx[step, :, 0:LANES] = qa[part * QB : (part + 1) * QB, :]
                qx[step, :, LANES : 2 * LANES] = pick
                gx[step] = ga[part * QB : (part + 1) * QB, :]
                gt[step] = gt4[a * CH : (a + 1) * CH, part * QB : (part + 1) * QB]
    dk[...] = jnp.zeros(dk.shape, f32)
    dv[...] = jnp.zeros(dv.shape, f32)
    chunks = [slice(c * KC, (c + 1) * KC) for c in range(KEYS // KC)]

    def item_of(step):
        return step // BLOCKS if rows else 0

    def score_chunk(step, bufs, c, top):
        s = dot(kx[item_of(step), c, :], qx[step], 1, 1)
        bufs[0][c, :] = s
        return jnp.maximum(top, jnp.max(s.reshape(KC // 8, 8, QB), axis=0))

    def expo_chunk(step, bufs, c, top, total):
        bufs[1][c, :] = dot(vx[item_of(step), c, :], gx[step], 1, 1)
        e = jnp.exp2((bufs[0][c, :] - top) * EXP2_SCALE)
        bufs[0][c, :] = e
        return total + jnp.sum(e.reshape(KC // 8, 8, QB), axis=0)

    def weight_chunk(step, bufs, c, inverse, out):
        w = (bufs[0][c, :] * inverse).astype(bf16)
        wl[c, :] = w
        return out + dot(vt[item_of(step), step % BLOCKS, :, c], w)

    def grad_chunk(step, bufs, c, inverse, delta, dq):
        item = item_of(step)
        ds = (bufs[0][c, :] * inverse * (bufs[1][c, :] - delta)).astype(bf16)
        dv[item, c, :] += dot(wl[c, :], gx[step])
        dk[item, c, :] += dot(ds, qx[step, :, 0:LANES])
        return dq + dot(kt[item, step % BLOCKS, :, c], ds)

    def fused(step, bufs, inverse, after, after_bufs):
        top = jnp.full((8, QB), -jnp.inf, f32)
        out = jnp.zeros((CH, QB), f32)
        for c in chunks:
            if after is not None:
                top = score_chunk(after, after_bufs, c, top)
            if step is not None:
                out = weight_chunk(step, bufs, c, inverse, out)
        top = jnp.max(top, axis=0, keepdims=True)
        if step is not None:
            delta = jnp.sum(gt[step] * out, axis=0, keepdims=True)
            scaled = inverse * SCALE
        total = jnp.zeros((8, QB), f32)
        dq = jnp.zeros((CH, QB), f32)
        for c in chunks:
            if step is not None:
                dq = grad_chunk(step, bufs, c, scaled, delta, dq)
            if after is not None:
                total = expo_chunk(after, after_bufs, c, top, total)
        if step is not None:
            dqt[step] = dq
        return 1.0 / jnp.sum(total, axis=0, keepdims=True)

    even, odd = (st, da), (st2, da2)

    def two_steps(pair, inverse):
        inverse = fused(2 * pair, even, inverse, 2 * pair + 1, odd)
        return fused(2 * pair + 1, odd, inverse, 2 * pair + 2, even)

    inverse = fused(None, None, None, 0, even)
    inverse = lax.fori_loop(0, 3, two_steps, inverse)
    inverse = fused(6, even, inverse, 7, odd)
    fused(7, odd, inverse, None, None)

    for item in range(items):
        dq4 = [
            dqt[(item + part) * BLOCKS : (item + part + 1) * BLOCKS].reshape(LANES, QB).T
            for part in range(group // QB)
        ]
        sums = [jnp.concatenate(dq4, axis=0) if len(dq4) > 1 else dq4[0]]
        for acc in (dk, dv):
            total = acc[item, 0:group, :]
            for d in range(1, turns):
                total += pltpu.roll(acc[item, d * group : (d + 1) * group, :], LANES - turn * d, 1)
            sums.append(total)
        for t in range(3):
            first = t * tensor_rows + item * 16
            block = sums[t].reshape(peers, 16, LANES).astype(bf16)
            if rows:
                out_ref[:, first : first + 16, :] = block
                continue
            for n in range(peers):
                source_y = (y_ref[0] + TURNS - n % TURNS) & (TURNS - 1)
                source = n // TURNS // 2 * 8 + source_y * 2 + n // TURNS % 2
                out_ref[source, first : first + 16, :] = block[n]


def attend(rows, y, received):
    items = 2 if rows else 1
    peers = 16 if rows else 32
    scratch = [
        pltpu.VMEM((8, QB, 2 * LANES), bf16),
        pltpu.VMEM((8, QB, LANES), bf16),
        pltpu.VMEM((8, CH, QB), f32),
        pltpu.VMEM((items, KEYS, 2 * LANES), bf16),
        pltpu.VMEM((items, BLOCKS, CH, KEYS), bf16),
        pltpu.VMEM((items, KEYS, LANES), bf16),
        pltpu.VMEM((items, BLOCKS, CH, KEYS), bf16),
        pltpu.VMEM((8, CH, QB), f32),
        pltpu.VMEM((items, KEYS, LANES), f32),
        pltpu.VMEM((items, KEYS, LANES), f32),
        pltpu.VMEM((KEYS, QB), f32),
        pltpu.VMEM((KEYS, QB), f32),
        pltpu.VMEM((KEYS, QB), f32),
        pltpu.VMEM((KEYS, QB), f32),
        pltpu.VMEM((KEYS, QB), bf16),
    ]
    out = jax.ShapeDtypeStruct((peers, 96 if rows else 48, LANES), bf16)
    spaces = [pltpu.SMEM, pltpu.VMEM]
    return call(functools.partial(attend_body, rows), out, scratch, y, received, spaces=spaces)


def regroup_body(*refs):
    out_hbm, tile_buf, sems = refs[TURNS:]
    sends = [
        pltpu.make_async_copy(
            refs[k].at[:, 0:64, :], out_hbm.at[:, k * 64 : (k + 1) * 64, :], sems.at[k]
        )
        for k in range(TURNS)
    ]
    sends.append(pltpu.make_async_copy(tile_buf, out_hbm.at[:, 256:264, :], sems.at[TURNS]))
    for send in sends[:TURNS]:
        send.start()
    row = iota((8, LANES), 0) // 2
    for w in range(8):
        tile = jnp.zeros((8, LANES), f32)
        for k in range(TURNS):
            tile = jnp.where(row == k, refs[k][w, 64:72, :].astype(f32), tile)
        tile_buf[w] = tile.astype(bf16)
    sends[TURNS].start()
    for send in sends:
        send.wait()


def unpack_rows_body(in_ref, out_ref, scr_ref):
    for t in range(3):
        scr_ref[t] = in_ref[:, t * 32 : (t + 1) * 32, :].reshape(512, LANES).astype(f32)
    for t in range(3):
        for l in range(16):
            out_ref[t, :, l * LANES : (l + 1) * LANES] = scr_ref[t, pl.ds(l, 32, stride=16), :]


def finish_body(rows_ref, in_ref, q_hbm, k_hbm, v_hbm, bufs, sems):
    low = iota((16, LANES), 1) < 64
    sends = [
        pltpu.make_async_copy(bufs.at[t], hbm, sems.at[t])
        for t, hbm in enumerate((q_hbm, k_hbm, v_hbm))
    ]
    for t in range(3):
        for l in range(16):
            cols = slice(l * LANES, (l + 1) * LANES)
            a = in_ref[2 * l, t * 16 : (t + 1) * 16, :].astype(f32)
            b = in_ref[2 * l + 1, t * 16 : (t + 1) * 16, :].astype(f32)
            upper = jnp.where(low, a, pltpu.roll(b, 64, 1))
            lower = jnp.where(low, pltpu.roll(a, 64, 1), b)
            bufs[t, 0:16, cols] = rows_ref[t, 0:16, cols] + upper
            bufs[t, 16:32, cols] = rows_ref[t, 16:32, cols] + lower
        sends[t].start()
    for send in sends:
        send.wait()


def exchange(array, axis, groups=None):
    return lax.all_to_all(
        array, axis, split_axis=0, concat_axis=0, tiled=True, axis_index_groups=groups
    )


def pack(y, *args):
    outs = [jax.ShapeDtypeStruct((16, 136, LANES), bf16)]
    outs += [jax.ShapeDtypeStruct((8, 72, LANES), bf16)] * TURNS
    scratch = [
        pltpu.VMEM((4, 32, 2048), bf16),
        pltpu.VMEM((32, 64), jnp.int32),
        pltpu.VMEM((4, 512, LANES), f32),
        pltpu.VMEM((4, 16, 32, LANES), bf16),
        pltpu.VMEM((16, 8, LANES), bf16),
        pltpu.SemaphoreType.DMA((5,)),
        pltpu.SemaphoreType.DMA((5,)),
    ]
    spaces = [pltpu.SMEM] + [pltpu.HBM] * 5
    out_spaces = [pl.BlockSpec(memory_space=m) for m in [pltpu.HBM] + [pltpu.VMEM] * TURNS]
    args = [pltpu.with_memory_space_constraint(a, pltpu.HBM) for a in args]
    return call(pack_body, outs, scratch, y, *args, spaces=spaces, out_spaces=out_spaces)


def regroup(arrays):
    scratch = [pltpu.VMEM((8, 8, LANES), bf16), pltpu.SemaphoreType.DMA((TURNS + 1,))]
    out = jax.ShapeDtypeStruct((8, 264, LANES), bf16)
    return call(regroup_body, out, scratch, *arrays, out_spaces=pl.BlockSpec(memory_space=pltpu.HBM))


def unpack_rows(array):
    out = jax.ShapeDtypeStruct((3, 32, 2048), f32)
    return call(unpack_rows_body, out, [pltpu.VMEM((3, 512, LANES), f32)], array)


def finish(row_part, array):
    scratch = [pltpu.VMEM((3, 32, 2048), f32), pltpu.SemaphoreType.DMA((3,))]
    outs = [jax.ShapeDtypeStruct((32, 2048), f32)] * 3
    out_spaces = [pl.BlockSpec(memory_space=pltpu.HBM)] * 3
    return call(finish_body, outs, scratch, row_part, array, out_spaces=out_spaces)


def along_y(k):
    return [(i, i - i % 8 + (i + 2 * k) % 8) for i in range(32)]


def per_device(*args):
    y = ((lax.axis_index("res") >> 1) & (TURNS - 1)).reshape(1)
    row_send, *col_send = pack(y, *args)
    turned = [col_send[0]] + [None] * 3
    for k in ORDER:
        turned[k] = lax.ppermute(col_send[k], "res", along_y(k))
    row_in = exchange(row_send, "prog")
    planes = [[x * 8 + y * 2 + c for x in range(4) for c in range(2)] for y in range(4)]
    col_in = exchange(regroup(turned), "res", planes)
    row_out = exchange(attend(True, y, row_in), "prog")
    col_out = exchange(attend(False, y, col_in), "res")
    return tuple(finish(unpack_rows(row_out), col_out))


def solution(mesh):
    return jax.shard_map(
        per_device,
        mesh=mesh,
        in_specs=(P("res", "prog"),) * 5,
        out_specs=(P("res", "prog"),) * 3,
        check_vma=False,
    )
```
